128 devices in a mesh: pair: 16 (over x, y_lo, core), cores: 8 (over z, y_hi).
Axes of the slice: x: 4, y: 4 (y_hi: 2, y_lo: 2; y = y_hi * 2 + y_lo), z: 4, core: 2. Of those that a mesh axis runs over, the one named last changes fastest.
Arguments:
- basis_rows: bfloat16 [32768, 2048], P('pair'), may hold values from -0.03125 to 0.03125
- energies: float32 [32768], P('pair'), may hold values from 0.5 to 4
- integrals: bfloat16 [32768, 4096], P('pair', 'cores'), may hold values from -0.75 to 0.75
- core_amps: bfloat16 [2048, 2048], P(('pair', 'cores')), may hold values from -3 to 3
- denominators: float32 [2048], replicated, may hold values from 1 to 4
Outputs:
- core_next: float32 [2048, 2048], P(('pair', 'cores'))
- amplitudes: bfloat16 [32768, 2048], P('pair')
The draws below stay inside these ranges and needn't reach their ends.
All inputs are finite; a program needn't handle non-finite values.
Results may differ from the reference program's by a relative error of at most 0.0056.
Values may be sent and summed in bfloat16 or wider, within the bound.
No kernel may reach another device: no remote copies, remote signals or barrier semaphores. Data moves between devices by JAX's collectives and lax.ppermute only.
A program may use at most 128 MiB of HBM per device.

```python
import math
import jax
import jax.numpy as jnp

R = 2048
NAUX = 4096
NOV = 32768


def level_of(rng, shape, shards, least, top_value):
    def one(dim, parts):
        draws = jax.random.uniform(jax.random.fold_in(jax.random.fold_in(rng, 6), dim), (parts,), jnp.float32, least / len(shards), top_value / len(shards))
        return jnp.repeat(jnp.exp(draws), shape[dim] // parts).reshape((-1,) + (1,) * (len(shape) - dim - 1))

    factor_of = one(*shards[0])
    for cut in shards[1:]:
        factor_of = factor_of * one(*cut)
    return factor_of


def gaussian(rng, extent, width, bound, pieces=(), dtype=jnp.bfloat16):
    values = width * jax.random.normal(rng, extent, jnp.float32)
    if pieces:
        values = values * level_of(rng, extent, pieces, -0.22, 0.18)
    return jnp.clip(values, -bound, bound).astype(dtype)


def setup_inputs(seed: int = 0) -> dict:
    arg_keys = jax.random.split(jax.random.key(seed), 6)
    return {
        "basis_rows": gaussian(arg_keys[0], (NOV, R), NOV ** -0.5, 0.03125, ((0, 16),)),
        "energies": jnp.clip(jnp.exp(math.log(4.0) - 2.0794415 * jax.random.uniform(arg_keys[1], (NOV,), jnp.float32) ** level_of(arg_keys[1], (NOV,), ((0, 16),), -0.2, 0.2)), 0.5, 4.0),
        "integrals": gaussian(arg_keys[2], (NOV, NAUX), (NAUX ** 0.5) ** -0.5, 0.75, ((0, 16), (1, 8))),
        "core_amps": gaussian(arg_keys[3], (R, R), 0.5, 3.0, ((0, 128),)),
        "denominators": jnp.clip(jnp.exp(jax.random.uniform(arg_keys[4], (R,), jnp.float32, math.log(1.0), math.log(4.0))), 1.0, 4.0),
    }


def reference(basis_rows, energies, integrals, core_amps, denominators):
    projected = jnp.dot(basis_rows.T, integrals, preferred_element_type=jnp.float32)
    projected_b = projected.astype(jnp.bfloat16)
    coulomb = jnp.dot(projected_b, projected_b.T, preferred_element_type=jnp.float32)
    weighted = (energies[:, None] * basis_rows.astype(jnp.float32)).astype(jnp.bfloat16)
    fock = jnp.dot(weighted.T, basis_rows, preferred_element_type=jnp.float32)
    fock_b = fock.astype(jnp.bfloat16)
    residual = coulomb + jnp.dot(fock_b, core_amps, preferred_element_type=jnp.float32)
    core_next = core_amps.astype(jnp.float32) - residual / (denominators[:, None] + denominators[None, :])
    core_b = core_next.astype(jnp.bfloat16)
    amplitudes = jnp.dot(basis_rows, core_b, preferred_element_type=jnp.float32).astype(jnp.bfloat16)
    return core_next, amplitudes
```

```python
import jax
import jax.numpy as jnp
import numpy as np
from jax import lax
from jax.experimental import pallas as pl
from jax.experimental.pallas import tpu as pltpu
from jax.sharding import Mesh, PartitionSpec as P

AXES = ("x", "yl", "k", "z", "yh")
SIZES = (4, 2, 2, 4, 2)
PAIR = ("x", "yl", "k")
CORES = ("z", "yh")
YC = ("yl", "k")
ORDER = (("y", "z", "x"), ("z", "x", "y"))


def contract_rows(left, right):
    return lax.dot_general(
        left, right, (((0,), (0,)), ((), ())), preferred_element_type=jnp.float32
    )


def shift_pairs(phase, step):
    pairs = []
    for index in np.ndindex(*SIZES):
        x, yl, k, z, yh = index
        at = {"x": x, "y": yh * 2 + yl, "z": z}
        axis = ORDER[k][phase]
        at[axis] = (at[axis] + step) % 4
        to = (at["x"], at["y"] % 2, k, at["z"], at["y"] // 2)
        pairs.append((int(np.ravel_multi_index(index, SIZES)), int(np.ravel_multi_index(to, SIZES))))
    return pairs


def swap_cores(value):
    return lax.ppermute(value, "k", [(0, 1), (1, 0)])


ROWS = 256


def multiply_kernel(place, basis_ref, *refs, aliased):
    parts = refs[:4]
    out_ref, core, out_buf, in_sem, out_sem = refs[4 + aliased :]
    step = pl.program_id(0)
    steps = pl.num_programs(0)
    at_x, at_y, at_z, which = place[0], place[1], place[2], place[3]

    def part_copy(first, second, third):
        def back(own, offset):
            return lax.rem(own - offset + 4, 4)

        x = jnp.where(which == 0, back(at_x, third), back(at_x, second))
        y = jnp.where(which == 0, back(at_y, first), back(at_y, third))
        z = jnp.where(which == 0, back(at_z, second), back(at_z, first))
        row = (z * 2 + y // 2) * 16
        column = (y % 2) * 512
        return pltpu.make_async_copy(
            parts[third].at[second, first],
            core.at[pl.ds(x * 4, 4), pl.ds(pl.multiple_of(row, 16), 16), pl.ds(pl.multiple_of(column, 512), 512)],
            in_sem.at[third * 16 + second * 4 + first],
        )

    offsets = [(a, b, c) for c in range(4) for b in range(4) for a in range(4)]

    @pl.when(step == 0)
    def _():
        for offset in offsets:
            part_copy(*offset).start()
        for offset in offsets:
            part_copy(*offset).wait()

    def out_copies(at, slot):
        return [
            pltpu.make_async_copy(
                out_buf.at[slot, :, pl.ds(tile * 128, 128)],
                out_ref.at[
                    pl.ds(pl.multiple_of(at * ROWS, ROWS), ROWS),
                    pl.ds(pl.multiple_of((tile % 4) * 512 + ((tile // 4) * 2 + which) * 128, 128), 128),
                ],
                out_sem.at[slot, tile],
            )
            for tile in range(8)
        ]

    slot = lax.rem(step, 2)

    @pl.when(step >= 2)
    def _():
        for copy in out_copies(step - 2, slot):
            copy.wait()

    for block in range(4):
        columns = pl.ds(block * 256, 256)
        right = core[:, :, columns].reshape(2048, 256)
        out_buf[slot, :, columns] = jnp.dot(
            basis_ref[...], right, preferred_element_type=jnp.float32
        ).astype(jnp.bfloat16)
    for copy in out_copies(step, slot):
        copy.start()

    @pl.when(step == steps - 1)
    def _():
        for copy in out_copies(step - 1, 1 - slot):
            copy.wait()
        for copy in out_copies(step, slot):
            copy.wait()


def multiply(place, basis_rows, parts, out=None):
    rows = basis_rows.shape[0]
    any_spec = pl.BlockSpec(memory_space=pl.ANY)
    aliased = 0 if out is None else 1
    extra = () if out is None else (out,)

    def kernel(*refs):
        multiply_kernel(*refs, aliased=aliased)

    return pl.pallas_call(
        kernel,
        out_shape=jax.ShapeDtypeStruct((rows, 2048), jnp.bfloat16),
        grid_spec=pltpu.PrefetchScalarGridSpec(
            num_scalar_prefetch=1,
            grid=(rows // ROWS,),
            in_specs=[pl.BlockSpec((ROWS, 2048), lambda i, place: (i, 0))] + [any_spec] * (4 + aliased),
            out_specs=any_spec,
            scratch_shapes=[
                pltpu.VMEM((16, 128, 1024), jnp.bfloat16),
                pltpu.VMEM((2, ROWS, 1024), jnp.bfloat16),
                pltpu.SemaphoreType.DMA((64,)),
                pltpu.SemaphoreType.DMA((2, 8)),
            ],
        ),
        input_output_aliases={6: 0} if aliased else {},
        cost_estimate=pl.CostEstimate(
            flops=2 * rows * 2048 * 1024, bytes_accessed=rows * 6144 + 2048 * 2048, transcendentals=0
        ),
        name="multiply",
    )(place, basis_rows, *parts, *extra)


def local(basis_rows, energies, integrals, core_amps, denominators):
    x, yl, k, z, yh = (lax.axis_index(a) for a in AXES)
    yc = yl * 2 + k
    c = z * 2 + yh
    f32, bf16 = jnp.float32, jnp.bfloat16

    sent = core_amps.reshape(16, 4, 4, 128).transpose(2, 0, 1, 3).reshape(1, 4, 16, 512)
    sent = jnp.broadcast_to(sent, (4, 4, 16, 512)).reshape(16, 16, 512)
    amps = lax.all_to_all(sent, PAIR, 0, 0, tiled=True).reshape(256, 512)

    projected = contract_rows(basis_rows, integrals).astype(bf16)
    at_column = lax.broadcasted_iota(jnp.int32, (2048, 256), 1)
    at_row = lax.broadcasted_iota(jnp.int32, (2048, 256), 0)
    pick = (at_row == (at_column // 16) * 128 + c * 16 + at_column % 16).astype(bf16)
    picked = jnp.dot(basis_rows, pick, preferred_element_type=f32).astype(bf16)
    weighted = (energies[:, None] * basis_rows.astype(f32)).astype(bf16)
    fock = contract_rows(weighted, picked).astype(bf16)
    both = jnp.concatenate([projected, fock], axis=1).reshape(16, 128, 768)
    both = lax.all_to_all(both, PAIR, 0, 0, tiled=True)
    both = jnp.sum(both.astype(f32), axis=0).astype(bf16)

    left = lax.all_gather(both, YC, axis=0, tiled=True)
    right = lax.all_gather(both[:, :512], "x", axis=0, tiled=True)
    term = lax.dot_general(
        left[:, :512], right, (((1,), (1,)), ((), ())), preferred_element_type=f32
    ) + jnp.dot(left[:, 512:], amps, preferred_element_type=f32)
    term = term.astype(bf16).reshape(4, 8, 16, 512).transpose(1, 0, 2, 3)
    term = lax.all_to_all(term, CORES, 0, 0, tiled=True)
    residual = jnp.sum(term.astype(f32), axis=0)

    own_amps = lax.dynamic_slice_in_dim(amps, x * 64, 64, 0).reshape(4, 16, 512)
    row_denoms = lax.dynamic_slice(denominators.reshape(4, 4, 8, 16), (x, 0, c, 0), (1, 4, 1, 16))
    column_denoms = lax.dynamic_slice(denominators.reshape(4, 4, 128), (0, yc, 0), (4, 1, 128))
    core = own_amps.astype(f32) - residual / (
        row_denoms.reshape(4, 16, 1) + column_denoms.reshape(1, 1, 512)
    )

    held = core.astype(bf16)
    for phase in range(2):
        held = jnp.stack([held] + [lax.ppermute(held, AXES, shift_pairs(phase, s)) for s in (1, 2, 3)])
    parts = [held] + [lax.ppermute(held, AXES, shift_pairs(2, s)) for s in (1, 2, 3)]
    others = [swap_cores(part) for part in parts]

    core_next = lax.all_to_all(core, YC, 0, 0, tiled=True)
    core_next = core_next.reshape(4, 16, 4, 128).transpose(1, 2, 0, 3).reshape(16, 2048)

    y = yh * 2 + yl
    amplitudes = multiply(jnp.stack([x, y, z, k]).astype(jnp.int32), basis_rows, parts)
    amplitudes = multiply(
        jnp.stack([x, y, z, 1 - k]).astype(jnp.int32), basis_rows, others, amplitudes
    )
    return (core_next, amplitudes)


def solution(mesh):
    fine = Mesh(mesh.devices.reshape(SIZES), AXES)
    in_specs = (P(PAIR, None), P(PAIR), P(PAIR, CORES), P(PAIR + CORES, None), P())
    out_specs = (P(PAIR + CORES, None), P(PAIR, None))
    return jax.shard_map(local, mesh=fine, in_specs=in_specs, out_specs=out_specs, check_vma=False)
```
